32 devices in a mesh: group: 4 (over y, x), member: 4 (over z), half: 2 (over core).
Axes of the slice: x: 2, y: 2, z: 4, core: 2. Of those that a mesh axis runs over, the one named last changes fastest.
Arguments:
- tokens: bfloat16 [2048, 2048], P(('group', 'member'), 'half'), may hold values from -6 to 6
- group_ids: int32 [2048, 1], P(('group', 'member')), may hold values from 0 to 3, as said below
- expert_ids: int32 [2, 2048, 4], P(None, ('group', 'member')), may hold values from 0 to 3, as said below
- gate_weights: bfloat16 [2, 2048, 4], P(None, ('group', 'member')), may hold values from 0.25 to 1
- w_gate: bfloat16 [16, 2048, 768], P(('group', 'member'), None, 'half'), may hold values from -0.125 to 0.125
- w_up: bfloat16 [16, 2048, 768], P(('group', 'member'), None, 'half'), may hold values from -0.125 to 0.125
- w_down: bfloat16 [16, 768, 2048], P(('group', 'member'), 'half'), may hold values from -0.21875 to 0.21875
Outputs:
- rows_out: bfloat16 [2048, 2048], P(('group', 'member'), 'half')
The draws below stay inside these ranges and needn't reach their ends.
Inputs may be any that keep to these rules, and one draw needn't show every extreme that they name: `group_ids`: in each aligned block of 128 rows (the rows of one device) at most 48 rows name the same group, and in every block some group is named by exactly 48 rows. `expert_ids`: each row names four different members. Among the rows of one device that name one group, in one pass, at most 48 name the same member; the rows of one device that take up all 48 slots of a group reach it. Every member is named by some row.
All inputs are finite; a program needn't handle non-finite values.
Results may differ from the reference program's by a relative error of at most 0.015.
Values may be sent and summed in bfloat16 or wider, within the bound.
No kernel may reach another device: no remote copies, remote signals or barrier semaphores. Data moves between devices by JAX's collectives and lax.ppermute only.
A program may use at most 64 MiB of HBM per device.

```python
import jax
import jax.numpy as jnp
from jax import lax

D = 2048
FF = 768
TOK_DEV = 128
PASSES = 2
EXPERTS = 16
TOKENS = 2048
CAP_G = 48
N_GROUP = 4
N_MEMBER = 4
N_HALF = 2


def routing(key):
    base = jax.random.fold_in(key, 7301)
    block_count = N_GROUP * N_MEMBER
    slot_total = N_GROUP * CAP_G
    key_hot, key_bias, key_score, key_order, key_perm = jax.random.split(base, 5)
    hot_member = jax.random.randint(key_hot, (N_MEMBER,), 0, N_GROUP)
    hot_block = jnp.tile(hot_member, N_GROUP)
    bias = jax.random.randint(key_bias, (N_GROUP,), 0, 4)
    label = jnp.arange(slot_total, dtype=jnp.int32) // CAP_G
    noise = jax.random.randint(key_score, (block_count, slot_total), 0, 1024)
    score = noise + bias[label][None, :] * 1024 + (label[None, :] == hot_block[:, None]).astype(jnp.int32) * 8192
    score = score * slot_total + jnp.arange(slot_total, dtype=jnp.int32)[None, :]
    unused, chosen = lax.top_k(score, TOK_DEV)
    order = jax.random.randint(key_order, (block_count, TOK_DEV), 0, 1 << 20) * TOK_DEV + jnp.arange(TOK_DEV, dtype=jnp.int32)[None, :]
    shuffle = jnp.argsort(order, axis=1)
    chosen = jnp.take_along_axis(chosen, shuffle, axis=1)
    groups = (chosen // CAP_G).astype(jnp.int32)
    onehot = (groups[:, :, None] == jnp.arange(N_GROUP, dtype=jnp.int32)[None, None, :]).astype(jnp.int32)
    before = jnp.cumsum(onehot, axis=1) - onehot
    ranking = jnp.sum(before * onehot, axis=2)
    perm_score = jax.random.randint(key_perm, (PASSES, block_count, N_GROUP, N_MEMBER), 0, 1 << 20) * N_MEMBER + jnp.arange(N_MEMBER, dtype=jnp.int32)
    members_perm = jnp.argsort(perm_score, axis=3).astype(jnp.int32)
    index = jnp.broadcast_to(groups[None, :, :, None], (PASSES, block_count, TOK_DEV, N_MEMBER))
    token_perm = jnp.take_along_axis(members_perm, index, axis=2)
    window = (4 * ranking[:, :, None] + jnp.arange(4, dtype=jnp.int32)[None, None, :]) % N_MEMBER
    window = jnp.broadcast_to(window[None], (PASSES, block_count, TOK_DEV, 4))
    picks = jnp.take_along_axis(token_perm, window, axis=3)
    return (groups.reshape(TOKENS, 1), picks.reshape(PASSES, TOKENS, 4).astype(jnp.int32))


def draw_group_ids(key, part):
    return routing(key)[0]


def draw_expert_ids(key, part):
    return routing(key)[1]


def levels(stream_key, dims, cuts, smallest, top_value):
    factor_of, own = 1.0, jax.random.fold_in(stream_key, 6)
    for dim, parts in cuts:
        steps = jnp.exp(jax.random.uniform(jax.random.fold_in(own, dim), (parts,), jnp.float32, smallest / len(cuts), top_value / len(cuts)))
        factor_of = factor_of * jnp.repeat(steps, dims[dim] // parts).reshape([-1 if axis == dim else 1 for axis in range(len(dims))])
    return factor_of


def gaussian(own_key, dims, width, reach, cuts=(), held_as=jnp.bfloat16):
    values = jax.random.normal(own_key, dims, jnp.float32) * width
    if len(cuts) > 0:
        values = levels(own_key, dims, cuts, -0.22, 0.18) * values
    return jnp.clip(values, min=-reach, max=reach).astype(held_as)


def setup_inputs(seed: int = 0) -> dict:
    splits = jax.random.split(jax.random.key(seed), 8)
    tokens = gaussian(splits[0], (TOKENS, D), 1.0, 6.0, ((0, 16), (1, 2)))
    group_ids = draw_group_ids(jax.random.fold_in(splits[7], 71), 0)
    expert_ids = draw_expert_ids(jax.random.fold_in(splits[7], 71), 0)
    gate_weights = jnp.clip(0.25 + 0.75 * jax.random.uniform(splits[3], (PASSES, TOKENS, 4), jnp.float32) ** levels(splits[3], (PASSES, TOKENS, 4), ((1, 16),), -0.2, 0.2), 0.25, 1.0).astype(jnp.bfloat16)
    w_gate = gaussian(splits[4], (EXPERTS, D, FF), D ** -0.5, 0.125, ((0, 16), (2, 2)))
    w_up = gaussian(splits[5], (EXPERTS, D, FF), D ** -0.5, 0.125, ((0, 16), (2, 2)))
    w_down = gaussian(splits[6], (EXPERTS, FF, D), FF ** -0.5, 0.21875, ((0, 16), (1, 2)))
    return dict(tokens=tokens, group_ids=group_ids, expert_ids=expert_ids, gate_weights=gate_weights, w_gate=w_gate, w_up=w_up, w_down=w_down)


epsilon = 1e-06

def expert_terms(rows, gates, weight_gate, weight_up, weight_down):
    pre_gate = jnp.dot(rows, weight_gate, preferred_element_type=jnp.float32)
    up_value = jnp.dot(rows, weight_up, preferred_element_type=jnp.float32)
    hidden = (jax.nn.silu(pre_gate) * up_value).astype(jnp.bfloat16)
    hidden_split = hidden.reshape(rows.shape[0], N_HALF, FF // N_HALF).astype(jnp.float32)
    down_split = weight_down.reshape(N_HALF, FF // N_HALF, D).astype(jnp.float32)
    halves_out = jnp.einsum('rhf,hfd->hrd', hidden_split, down_split)
    rounded = (halves_out * gates[None, :, None]).astype(jnp.bfloat16)
    rounded = lax.optimization_barrier(rounded)
    return lax.optimization_barrier(jnp.sum(rounded.astype(jnp.float32), axis=0))

def group_pass(rows, table, gate_all, up_all, down_all):

    def add_expert(carry, pieces):
        weight_gate, weight_up, weight_down, column = pieces
        return (carry + expert_terms(rows, column, weight_gate, weight_up, weight_down), None)
    start_total = jnp.zeros((rows.shape[0], D), jnp.float32)
    totals, unused = lax.scan(add_expert, start_total, (gate_all, up_all, down_all, table.T))
    lifted = rows.astype(jnp.float32) + totals
    factor = lax.rsqrt(lax.optimization_barrier(jnp.mean(lifted * lifted, axis=1, keepdims=True)) + epsilon)
    return (lifted * factor).astype(jnp.bfloat16)

def reference(tokens, group_ids, expert_ids, gate_weights, w_gate, w_up, w_down):
    token_count = tokens.shape[0]
    slot_count = N_GROUP * CAP_G
    group_rows = N_MEMBER * slot_count
    route_group = group_ids[:, 0].astype(jnp.int32)
    anchor = jnp.arange(token_count, dtype=jnp.int32) // TOK_DEV
    from_group = anchor // N_MEMBER
    from_member = anchor % N_MEMBER
    onehot = (route_group[:, None] == jnp.arange(N_GROUP, dtype=jnp.int32)[None, :]).astype(jnp.int32)
    blocks = onehot.reshape(-1, TOK_DEV, N_GROUP)
    before = (jnp.cumsum(blocks, axis=1) - blocks).reshape(token_count, N_GROUP)
    ranking = lax.optimization_barrier(jnp.sum(before * onehot, axis=1))
    position = (from_member * slot_count + from_group * CAP_G + ranking).astype(jnp.int32)
    stream = jnp.zeros((N_GROUP, group_rows, D), jnp.bfloat16).at[route_group, position].set(tokens)
    member_ids = jnp.arange(N_MEMBER, dtype=jnp.int32)
    dense_gates = lax.optimization_barrier(jnp.sum(gate_weights.astype(jnp.float32)[..., None] * (expert_ids[..., None] == member_ids).astype(jnp.float32), axis=2))
    gate_table = jnp.zeros((PASSES, N_GROUP, group_rows, N_MEMBER), jnp.float32).at[:, route_group, position].set(dense_gates)
    gates_all = w_gate.reshape(N_GROUP, N_MEMBER, D, FF)
    ups_all = w_up.reshape(N_GROUP, N_MEMBER, D, FF)
    downs_all = w_down.reshape(N_GROUP, N_MEMBER, FF, D)
    for pass_index in range(PASSES):
        stream = lax.map(lambda pieces: group_pass(*pieces), (stream, gate_table[pass_index], gates_all, ups_all, downs_all))
    return stream[route_group, position]
```

```python
import jax
import jax.numpy as jnp
from jax import lax
from jax.sharding import PartitionSpec as P

epsilon = 1e-06


def ring_order(count):
    return [0] + list(range(1, count, 2)) + list(range(count - 2 + count % 2, 0, -2))


def swap_halves(part, halves):
    return lax.ppermute(part, "half", [(i, halves - 1 - i) for i in range(halves)])


def exchange_groups(slabs, groups):
    return [slabs[0]] + [
        lax.ppermute(slabs[k], "group", [(i, i ^ k) for i in range(groups)])
        for k in range(1, groups)
    ]


def on_device(tokens, group_ids, expert_ids, gate_weights, w_gate, w_up, w_down):
    groups = lax.axis_size("group")
    members = lax.axis_size("member")
    halves = lax.axis_size("half")
    tok_rows, half_width = tokens.shape
    full_width = half_width * halves
    capacity = 3 * tok_rows // (2 * groups)
    part_cap = capacity // halves
    slot_count = groups * capacity
    rows = slot_count // halves
    passes = expert_ids.shape[0]
    own_group = lax.axis_index("group")
    own_member = lax.axis_index("member")
    own_half = lax.axis_index("half")
    order = ring_order(members)
    ring = [(order[i], order[(i + 1) % members]) for i in range(members)]

    weights = [(w_gate[0], w_up[0], w_down[0])]
    weights.append(tuple(swap_halves(w, halves) for w in weights[0]))

    column_ids = jnp.arange(groups, dtype=jnp.int32)
    onehot = (group_ids == column_ids[None, :]).astype(jnp.int32)
    before = jnp.cumsum(onehot, axis=0) - onehot
    rank = jnp.sum(before * onehot, axis=1)
    share = (rank // part_cap) ^ own_half
    target = share * rows + (group_ids[:, 0] ^ own_group) * part_cap + rank % part_cap
    placing = jnp.arange(slot_count, dtype=jnp.int32)[:, None] == target[None, :]
    send_rows = jnp.dot(
        placing.astype(jnp.bfloat16), tokens, preferred_element_type=jnp.float32
    ).astype(jnp.bfloat16)
    mine, theirs = send_rows[:rows], swap_halves(send_rows[rows:], halves)
    wide = jnp.where(
        own_half == 0,
        jnp.concatenate([mine, theirs], axis=1),
        jnp.concatenate([theirs, mine], axis=1),
    )
    landed = exchange_groups(
        [wide[k * part_cap : (k + 1) * part_cap] for k in range(groups)], groups
    )
    stream = jnp.concatenate(landed, axis=0)

    member_ids = jnp.arange(members, dtype=jnp.int32)
    dense_gates = jnp.sum(
        gate_weights.astype(jnp.float32)[..., None]
        * (expert_ids[..., None] == member_ids).astype(jnp.float32),
        axis=2,
    )
    dense_gates = jnp.transpose(dense_gates, (0, 2, 1)).reshape(passes * members, tok_rows)
    send_gates = lax.dot_general(
        dense_gates.astype(jnp.bfloat16),
        placing[:rows].astype(jnp.bfloat16),
        (((1,), (1,)), ((), ())),
        preferred_element_type=jnp.float32,
    ).astype(jnp.bfloat16)
    gate_slabs = exchange_groups(
        [send_gates[:, k * part_cap : (k + 1) * part_cap] for k in range(groups)], groups
    )
    gate_table = jnp.concatenate(gate_slabs, axis=1).reshape(passes, members, rows)
    order_ids = jnp.array(order, dtype=jnp.int32)
    place = jnp.sum(jnp.where(order_ids == own_member, member_ids, 0))
    gates = []
    for step in range(members):
        ahead = lax.rem(place + step, members)
        taker = jnp.sum(jnp.where(member_ids == ahead, order_ids, 0))
        picked = jnp.sum(
            jnp.where((member_ids == taker)[None, :, None], gate_table, 0), axis=1
        )
        if step > 0:
            picked = lax.ppermute(
                picked,
                "member",
                [(order[i], order[(i + step) % members]) for i in range(members)],
            )
        gates.append(picked)

    def term(block, gate):
        total = None
        for gate_w, up_w, down_w in weights:
            pre_gate = jnp.dot(block, gate_w, preferred_element_type=jnp.float32)
            up_value = jnp.dot(block, up_w, preferred_element_type=jnp.float32)
            hidden = (jax.nn.silu(pre_gate) * up_value).astype(jnp.bfloat16)
            projected = jnp.dot(hidden, down_w, preferred_element_type=jnp.float32)
            total = projected if total is None else total + projected
        return total * gate.astype(jnp.float32)[:, None]

    for pass_index in range(passes):
        block, carried = stream, None
        for step in range(1, members):
            block = lax.ppermute(block, "member", ring)
            part = term(block, gates[step][pass_index])
            if carried is not None:
                part = part + carried.astype(jnp.float32)
            carried = lax.ppermute(part.astype(jnp.bfloat16), "member", ring)
        lifted = stream.astype(jnp.float32) + term(stream, gates[0][pass_index])
        if carried is not None:
            lifted = lifted + carried.astype(jnp.float32)
        squares = jnp.sum(lifted * lifted, axis=1, keepdims=True)
        stream = (lifted * lax.rsqrt(squares / full_width + epsilon)).astype(jnp.bfloat16)

    back = jnp.concatenate(
        exchange_groups(
            [stream[k * part_cap : (k + 1) * part_cap] for k in range(groups)], groups
        ),
        axis=0,
    )
    left, right = back[:, :half_width], back[:, half_width:]
    kept = jnp.where(own_half == 0, left, right)
    given = swap_halves(jnp.where(own_half == 0, right, left), halves)
    result = lax.dot_general(
        placing.astype(jnp.bfloat16),
        jnp.concatenate([kept, given], axis=0),
        (((0,), (0,)), ((), ())),
        preferred_element_type=jnp.float32,
    )
    return result.astype(jnp.bfloat16)


def solution(mesh):
    placed = (
        P(("group", "member"), "half"),
        P(("group", "member"), None),
        P(None, ("group", "member"), None),
        P(None, ("group", "member"), None),
        P(("group", "member"), None, "half"),
        P(("group", "member"), None, "half"),
        P(("group", "member"), "half", None),
    )
    return jax.shard_map(
        on_device,
        mesh=mesh,
        in_specs=placed,
        out_specs=P(("group", "member"), "half"),
        check_vma=False,
    )
```

```python
import jax
import jax.numpy as jnp
from jax import lax
from jax.experimental import pallas as pl
from jax.experimental.pallas import tpu as pltpu
from jax.sharding import PartitionSpec as P

epsilon = 1e-06


def ring_order(count):
    return [0] + list(range(1, count, 2)) + list(range(count - 2 + count % 2, 0, -2))


def swap_halves(part, halves):
    return lax.ppermute(part, "half", [(i, halves - 1 - i) for i in range(halves)])


def exchange_groups(slabs, groups):
    return [slabs[0]] + [
        lax.ppermute(slabs[k], "group", [(i, i ^ k) for i in range(groups)])
        for k in range(1, groups)
    ]


def expert_kernel(x, gate, *refs):
    *weights, out = refs
    total = None
    for i in range(0, len(weights), 3):
        gate_w, up_w, down_w = weights[i : i + 3]
        pre_gate = jnp.dot(x[...], gate_w[...], preferred_element_type=jnp.float32)
        up_value = jnp.dot(x[...], up_w[...], preferred_element_type=jnp.float32)
        hidden = (jax.nn.silu(pre_gate) * up_value).astype(jnp.bfloat16)
        projected = jnp.dot(hidden, down_w[...], preferred_element_type=jnp.float32)
        total = projected if total is None else total + projected
    out[...] = total * gate[...].astype(jnp.float32)


def expert_term(x, gate, weights):
    flat = [w for three in weights for w in three]
    rows, width = x.shape
    inner = sum(three[0].shape[1] for three in weights)
    return pl.pallas_call(
        expert_kernel,
        out_shape=jax.ShapeDtypeStruct((rows, width), jnp.float32),
        in_specs=[pl.BlockSpec(memory_space=pltpu.VMEM)] * (2 + len(flat)),
        out_specs=pl.BlockSpec(memory_space=pltpu.VMEM),
        compiler_params=pltpu.CompilerParams(vmem_limit_bytes=24 * 1024 * 1024),
        cost_estimate=pl.CostEstimate(
            flops=6 * rows * width * inner, transcendentals=rows * inner, bytes_accessed=8 * rows * width
        ),
    )(x, gate, *flat)


def on_device(tokens, group_ids, expert_ids, gate_weights, w_gate, w_up, w_down):
    groups = lax.axis_size("group")
    members = lax.axis_size("member")
    halves = lax.axis_size("half")
    tok_rows, half_width = tokens.shape
    full_width = half_width * halves
    capacity = 3 * tok_rows // (2 * groups)
    part_cap = capacity // halves
    slot_count = groups * capacity
    rows = slot_count // halves
    passes = expert_ids.shape[0]
    own_group = lax.axis_index("group")
    own_member = lax.axis_index("member")
    own_half = lax.axis_index("half")
    order = ring_order(members)
    ring = [(order[i], order[(i + 1) % members]) for i in range(members)]

    weights = [(w_gate[0], w_up[0], w_down[0])]
    weights.append(tuple(swap_halves(w, halves) for w in weights[0]))

    column_ids = jnp.arange(groups, dtype=jnp.int32)
    onehot = (group_ids == column_ids[None, :]).astype(jnp.int32)
    before = jnp.cumsum(onehot, axis=0) - onehot
    rank = jnp.sum(before * onehot, axis=1)
    share = (rank // part_cap) ^ own_half
    target = share * rows + (group_ids[:, 0] ^ own_group) * part_cap + rank % part_cap
    placing = jnp.arange(slot_count, dtype=jnp.int32)[:, None] == target[None, :]
    send_rows = jnp.dot(
        placing.astype(jnp.bfloat16), tokens, preferred_element_type=jnp.float32
    ).astype(jnp.bfloat16)
    mine, theirs = send_rows[:rows], swap_halves(send_rows[rows:], halves)
    wide = jnp.where(
        own_half == 0,
        jnp.concatenate([mine, theirs], axis=1),
        jnp.concatenate([theirs, mine], axis=1),
    )
    landed = exchange_groups(
        [wide[k * part_cap : (k + 1) * part_cap] for k in range(groups)], groups
    )
    stream = jnp.concatenate(landed, axis=0)

    member_ids = jnp.arange(members, dtype=jnp.int32)
    dense_gates = jnp.sum(
        gate_weights.astype(jnp.float32)[..., None]
        * (expert_ids[..., None] == member_ids).astype(jnp.float32),
        axis=2,
    )
    dense_gates = jnp.transpose(dense_gates, (0, 2, 1)).reshape(passes * members, tok_rows)
    send_gates = lax.dot_general(
        dense_gates.astype(jnp.bfloat16),
        placing[:rows].astype(jnp.bfloat16),
        (((1,), (1,)), ((), ())),
        preferred_element_type=jnp.float32,
    ).astype(jnp.bfloat16)
    gate_slabs = exchange_groups(
        [send_gates[:, k * part_cap : (k + 1) * part_cap] for k in range(groups)], groups
    )
    gate_table = jnp.concatenate(gate_slabs, axis=1).reshape(passes, members, rows)
    order_ids = jnp.array(order, dtype=jnp.int32)
    place = jnp.sum(jnp.where(order_ids == own_member, member_ids, 0))
    gates = []
    for step in range(members):
        ahead = lax.rem(place + step, members)
        taker = jnp.sum(jnp.where(member_ids == ahead, order_ids, 0))
        picked = jnp.sum(
            jnp.where((member_ids == taker)[None, :, None], gate_table, 0), axis=1
        )
        if step > 0:
            picked = lax.ppermute(
                picked,
                "member",
                [(order[i], order[(i + step) % members]) for i in range(members)],
            )
        gates.append(picked)

    def term(block, gate):
        return expert_term(block, gate[:, None], weights)

    for pass_index in range(passes):
        block, carried = stream, None
        for step in range(1, members):
            block = lax.ppermute(block, "member", ring)
            part = term(block, gates[step][pass_index])
            if carried is not None:
                part = part + carried.astype(jnp.float32)
            carried = lax.ppermute(part.astype(jnp.bfloat16), "member", ring)
        lifted = stream.astype(jnp.float32) + term(stream, gates[0][pass_index])
        if carried is not None:
            lifted = lifted + carried.astype(jnp.float32)
        squares = jnp.sum(lifted * lifted, axis=1, keepdims=True)
        stream = (lifted * lax.rsqrt(squares / full_width + epsilon)).astype(jnp.bfloat16)

    back = jnp.concatenate(
        exchange_groups(
            [stream[k * part_cap : (k + 1) * part_cap] for k in range(groups)], groups
        ),
        axis=0,
    )
    left, right = back[:, :half_width], back[:, half_width:]
    kept = jnp.where(own_half == 0, left, right)
    given = swap_halves(jnp.where(own_half == 0, right, left), halves)
    result = lax.dot_general(
        placing.astype(jnp.bfloat16),
        jnp.concatenate([kept, given], axis=0),
        (((0,), (0,)), ((), ())),
        preferred_element_type=jnp.float32,
    )
    return result.astype(jnp.bfloat16)


def solution(mesh):
    placed = (
        P(("group", "member"), "half"),
        P(("group", "member"), None),
        P(None, ("group", "member"), None),
        P(None, ("group", "member"), None),
        P(("group", "member"), None, "half"),
        P(("group", "member"), None, "half"),
        P(("group", "member"), "half", None),
    )
    return jax.shard_map(
        on_device,
        mesh=mesh,
        in_specs=placed,
        out_specs=P(("group", "member"), "half"),
        check_vma=False,
    )
```

```python
import functools

import jax
import jax.numpy as jnp
from jax import lax
from jax.experimental import pallas as pl
from jax.experimental.pallas import tpu as pltpu
from jax.sharding import PartitionSpec as P

epsilon = 1e-06
lanes = 128


bf16 = jnp.bfloat16
f32 = jnp.float32
i32 = jnp.int32
in_vmem = pl.BlockSpec(memory_space=pltpu.VMEM)
in_smem = pl.BlockSpec(memory_space=pltpu.SMEM)


def call(kernel, out_shape, args, flops=0, moved=0, limit_mib=24):
    many = isinstance(out_shape, (list, tuple))
    return pl.pallas_call(
        kernel,
        out_shape=out_shape,
        in_specs=[in_smem] + [in_vmem] * (len(args) - 1),
        out_specs=[in_vmem] * len(out_shape) if many else in_vmem,
        compiler_params=pltpu.CompilerParams(vmem_limit_bytes=limit_mib * 1024 * 1024),
        cost_estimate=pl.CostEstimate(flops=flops, transcendentals=0, bytes_accessed=moved),
    )(*args)


def ring_order(count):
    return [0] + list(range(1, count, 2)) + list(range(count - 2 + count % 2, 0, -2))


def dot_t(a, b, a_dim, b_dim):
    return lax.dot_general(
        a, b, (((a_dim,), (b_dim,)), ((), ())), preferred_element_type=f32
    )


def joined(refs, width):
    parts = [ref[:, :width] for ref in refs]
    return parts[0] if len(parts) == 1 else jnp.concatenate(parts, axis=0)


def route_kernel(dims, here, tok, gid, eid, gate, out):
    groups, members, halves, part_cap, rows = dims
    passes, picks, count = eid.shape
    width = tok.shape[1]
    own_group, own_half = here[0], here[1]
    ids = gid[...]
    at_group = lax.broadcasted_iota(i32, (max(8, groups), count), 0) == ids
    onehot = jnp.where(at_group, 1.0, 0.0).astype(f32)
    row = lax.broadcasted_iota(i32, (count, count), 0)
    col = lax.broadcasted_iota(i32, (count, count), 1)
    earlier = jnp.where(row < col, 1.0, 0.0).astype(bf16)
    before = jnp.dot(onehot.astype(bf16), earlier, preferred_element_type=f32)
    rank = jnp.sum(before * onehot, axis=0, keepdims=True).astype(i32)
    share = jnp.zeros_like(rank)
    for k in range(1, halves):
        share = share + jnp.where(rank >= k * part_cap, 1, 0)
    target = (
        (share ^ own_half) * rows + (ids ^ own_group) * part_cap + rank - share * part_cap
    )
    line = lax.broadcasted_iota(i32, (lanes, count), 0)
    meta = jnp.where(line == passes * members, target.astype(f32), 0.0)
    for p in range(passes):
        chosen, weight = eid[p], gate[p].astype(f32)
        for k in range(picks):
            hit = line == chosen[k : k + 1] + p * members
            meta = meta + jnp.where(hit, weight[k : k + 1], 0.0)
    same = jnp.where(row == col, 1.0, 0.0).astype(bf16)
    out[:, :width] = tok[...]
    out[:, width:] = dot_t(same, meta.astype(bf16), 1, 1).astype(bf16)


def slot_column(meta, line):
    at = lax.broadcasted_iota(i32, meta.shape, 1) == line
    return jnp.sum(jnp.where(at, meta.astype(f32), 0.0), axis=1, keepdims=True)


def place_kernel(dims, here, mine, other, *outs):
    line, rows = dims
    count = mine.shape[0]
    width = mine.shape[1] - lanes
    half = here[1]
    slot = slot_column(mine[:, width:], line)
    spot = lax.broadcasted_iota(i32, (count, rows), 1).astype(f32) == slot
    spot = jnp.where(spot, 1.0, 0.0).astype(bf16)
    near = dot_t(spot, mine[...], 0, 0).astype(bf16)
    far = dot_t(spot, other[:, :width], 0, 0).astype(bf16)
    size = outs[0].shape[0]
    at_near = pl.multiple_of(half * width, lanes)
    at_far = pl.multiple_of((1 - half) * width, lanes)
    for k, out in enumerate(outs):
        part = slice(k * size, (k + 1) * size)
        out[:, pl.ds(at_near, width)] = near[part, :width]
        out[:, pl.ds(at_far, width)] = far[part]
        out[:, 2 * width :] = near[part, width:]


def expert(x, gate, weights):
    total = None
    for i in range(0, len(weights), 3):
        gate_w, up_w, down_w = weights[i : i + 3]
        pre_gate = jnp.dot(x, gate_w[...], preferred_element_type=f32)
        up_value = jnp.dot(x, up_w[...], preferred_element_type=f32)
        hidden = (jax.nn.silu(pre_gate) * up_value).astype(bf16)
        projected = jnp.dot(hidden, down_w[...], preferred_element_type=f32)
        total = projected if total is None else total + projected
    return total * gate


def gate_of(slabs, width, here, base):
    parts = [ref[:, width:].astype(f32) for ref in slabs]
    meta = parts[0] if len(parts) == 1 else jnp.concatenate(parts, axis=0)
    at = lax.broadcasted_iota(i32, meta.shape, 1) == here[2] + base
    return jnp.sum(jnp.where(at, meta, 0.0), axis=1, keepdims=True)


def first_kernel(dims, here, *refs):
    pieces, base, width, carry, count = dims
    slabs, refs = refs[:pieces], refs[pieces:]
    weights, refs = refs[:count], refs[count:]
    out = refs[-1]
    term = expert(joined(slabs, width), gate_of(slabs, width, here, base), weights)
    if carry:
        term = term + refs[0][...].astype(f32)
    out[...] = term.astype(out.dtype)


def norm_kernel(dims, here, *refs):
    pieces, width, carry = dims
    slabs, term, out = refs[:pieces], refs[pieces], refs[-1]
    lifted = joined(slabs, width).astype(f32) + term[...]
    if carry:
        lifted = lifted + refs[pieces + 1][...].astype(f32)
    squares = jnp.sum(lifted * lifted, axis=1, keepdims=True)
    out[...] = (lifted * lax.rsqrt(squares / width + epsilon)).astype(out.dtype)


def later_kernel(dims, here, x, *refs):
    pieces, base, width, own, count = dims
    slabs, weights = refs[:pieces], refs[pieces : pieces + count]
    outs = refs[pieces + count :]
    term = expert(x[...], gate_of(slabs, width, here, base), weights)
    if own:
        term = term + x[...].astype(f32)
    term = term.astype(bf16)
    size = outs[0].shape[0]
    for k, out in enumerate(outs):
        out[...] = term[k * size : (k + 1) * size]


def give_kernel(here, *refs):
    slabs, out = refs[:-1], refs[-1]
    width = out.shape[1]
    size = slabs[0].shape[0]
    at = pl.multiple_of((1 - here[1]) * width, lanes)
    for k, slab in enumerate(slabs):
        out[k * size : (k + 1) * size, :] = slab[:, pl.ds(at, width)]


def combine_kernel(dims, here, *refs):
    pieces, line, carry, last = dims
    slabs, refs = refs[:pieces], refs[pieces:]
    got, block, refs = refs[0], refs[1], refs[2:]
    width = got.shape[1]
    at = pl.multiple_of(here[1] * width, lanes)
    rows = jnp.concatenate([slab[:, pl.ds(at, width)] for slab in slabs] + [got[...]], axis=0)
    slot = slot_column(block[:, width:], line)
    spot = lax.broadcasted_iota(i32, (block.shape[0], rows.shape[0]), 1).astype(f32) == slot
    spot = jnp.where(spot, 1.0, 0.0).astype(bf16)
    total = jnp.dot(spot, rows, preferred_element_type=f32)
    if carry:
        total = total + refs[0][...].astype(f32)
    if last:
        out, squares = refs[-2:]
        sums = jnp.sum(total * total, axis=1, keepdims=True)
        squares[...] = jnp.broadcast_to(sums, squares.shape)
    else:
        out = refs[-1]
    out[...] = total.astype(out.dtype)


def finish_kernel(full_width, here, lifted, mine, other, out):
    squares = (mine[...] + other[...])[:, :1]
    out[...] = (lifted[...] * lax.rsqrt(squares / full_width + epsilon)).astype(out.dtype)


def on_device(tokens, group_ids, expert_ids, gate_weights, w_gate, w_up, w_down):
    groups = lax.axis_size("group")
    members = lax.axis_size("member")
    halves = lax.axis_size("half")
    count, half_width = tokens.shape
    width = half_width * halves
    capacity = 3 * count // (2 * groups)
    part_cap = capacity // halves
    slots = groups * capacity
    rows = slots // halves
    passes = expert_ids.shape[0]
    line = passes * members
    assert halves == 2 and passes == 2 and slots <= 256 and line < lanes
    order = ring_order(members)
    ring = [(order[i], order[(i + 1) % members]) for i in range(members)]
    here = jnp.stack(
        [lax.axis_index("group"), lax.axis_index("half"), lax.axis_index("member")]
    ).astype(i32)
    whole_slabs = part_cap % 8 != 0
    pieces = 1 if whole_slabs else groups
    slab_rows = rows // pieces

    def shape(*dims, dtype=bf16):
        return jax.ShapeDtypeStruct(dims, dtype)

    def swap(part):
        return lax.ppermute(part, "half", [(i, halves - 1 - i) for i in range(halves)])

    def turn(part):
        return lax.ppermute(part, "member", ring)

    def exchange(slabs):
        if whole_slabs:
            slabs = [slabs[0][k * part_cap : (k + 1) * part_cap] for k in range(groups)]
        got = [slabs[0]] + [
            lax.ppermute(slabs[k], "group", [(i, i ^ k) for i in range(groups)])
            for k in range(1, groups)
        ]
        return [jnp.concatenate(got, axis=0)] if whole_slabs else got

    own = (w_gate[0], w_up[0], w_down[0])
    weights = [*own, *(swap(w) for w in own)]
    inner = 2 * own[0].shape[1]
    work = 6 * rows * width * inner

    block = call(
        functools.partial(route_kernel, (groups, members, halves, part_cap, rows)),
        shape(count, half_width + lanes),
        (
            here,
            tokens,
            group_ids.reshape(1, count),
            jnp.transpose(expert_ids, (0, 2, 1)),
            jnp.transpose(gate_weights, (0, 2, 1)),
        ),
        moved=4 * count * half_width,
    )

    blocks = [block]
    for step in range(1, members):
        blocks.append(turn(blocks[-1]))
    tables = []
    for block in blocks:
        placed = call(
            functools.partial(place_kernel, (line, rows)),
            [shape(slab_rows, width + lanes)] * pieces,
            (here, block, swap(block)),
            flops=4 * count * rows * width,
            moved=4 * count * width,
        )
        tables.append(exchange(placed))

    def first(step, carried, dtype):
        extra = () if carried is None else (carried,)
        return call(
            functools.partial(
                first_kernel, (pieces, 0, width, carried is not None, len(weights))
            ),
            shape(rows, width, dtype=dtype),
            (here, *tables[step], *weights, *extra),
            flops=work,
            moved=8 * rows * width,
        )

    carried = None
    for step in range(1, members):
        carried = turn(first(step, carried, bf16))
    term = first(0, None, f32)
    extra = () if carried is None else (carried,)
    stream = call(
        functools.partial(norm_kernel, (pieces, width, carried is not None)),
        shape(rows, width),
        (here, *tables[0], term, *extra),
        moved=8 * rows * width,
    )

    x, carried, result = stream, None, None
    for step in [*range(1, members), 0]:
        x = turn(x) if step else stream
        out = call(
            functools.partial(
                later_kernel, (pieces, members, width, step == 0, len(weights))
            ),
            [shape(slab_rows, width)] * pieces,
            (here, x, *tables[step], *weights),
            flops=work,
            moved=8 * rows * width,
        )
        slabs = exchange(out)
        given = swap(
            call(give_kernel, shape(rows, half_width), (here, *slabs), moved=2 * rows * width)
        )
        extra = () if carried is None else (carried,)
        kinds = [shape(count, half_width)]
        if step == 0:
            kinds = [shape(count, half_width, dtype=f32), shape(count, lanes, dtype=f32)]
        made = call(
            functools.partial(combine_kernel, (pieces, line, carried is not None, step == 0)),
            kinds,
            (here, *slabs, given, blocks[step], *extra),
            flops=2 * count * slots * half_width,
            moved=8 * count * half_width,
        )
        if step:
            carried = turn(made[0])
        else:
            result = made
    lifted, squares = result
    return call(
        functools.partial(finish_kernel, width),
        shape(count, half_width),
        (here, lifted, squares, swap(squares)),
        moved=6 * count * half_width,
    )


def solution(mesh):
    placed = (
        P(("group", "member"), "half"),
        P(("group", "member"), None),
        P(None, ("group", "member"), None),
        P(None, ("group", "member"), None),
        P(("group", "member"), None, "half"),
        P(("group", "member"), None, "half"),
        P(("group", "member"), "half", None),
    )
    return jax.shard_map(
        on_device,
        mesh=mesh,
        in_specs=placed,
        out_specs=P(("group", "member"), "half"),
        check_vma=False,
    )
```
